512 devices in a mesh: region: 128 (over z, y, core), hour: 4 (over x).
Axes of the slice: x: 4, y: 8, z: 8, core: 2. Of those that a mesh axis runs over, the one named last changes fastest.
Arguments:
- kkt_inverse: bfloat16 [128, 1024, 1024], P('region'), may hold values from -1 to 2
- demand: float32 [512, 131072], P('hour', 'region'), may hold values from -6 to 6
- cost_quad: float32 [131072], P('region'), may hold values from 0.1 to 2
- cost_lin: float32 [131072], P('region'), may hold values from -1 to 1
- capacity: float32 [131072], P('region'), may hold values from 0.2 to 2
- ramp: float32 [131072], P('region'), may hold values from 0.05 to 1
- gen_start: float32 [131072], P('region'), may hold values from 0 to 1
- boundary_bus: int32 [128, 2, 128], P('region'), may hold values from 0 to 1023
- tie_count: int32 [128], replicated, may hold values from 32 to 128, as said below
- part_bus: int32 [1024, 8], replicated, may hold values from 0 to 131071
- part_share: float32 [1024, 8], replicated, may hold values from 0.05 to 1
- cleared_mw: float32 [4, 128, 1024], P('hour', 'region'), may hold values from -6 to 6
Outputs:
- angles: float32 [512, 131072], P('hour', 'region')
- payment: float32 [4, 128, 1024], P('hour', 'region')
The draws below stay inside these ranges and needn't reach their ends.
Inputs may be any that keep to these rules, and one draw needn't show every extreme that they name: Tie lines pair up in order: slots below tie_count[r] of region r's right block meet the same slots of the next region's left block (the last region's next is region 0); some region has 128 live tie lines.
All inputs are finite; a program needn't handle non-finite values.
Results may differ from the reference program's by a relative error of at most 0.0062.
Values may be sent and summed in bfloat16 or wider, within the bound.
A program may use at most 64 MiB of HBM per device.

```python
import math
import jax
import jax.numpy as jnp
import numpy as np
from jax import lax

B = 1024
NS = 128
PARTS_SIZE = 1024
TAPS = 8
ITERS = 2
H_DEV = 128
REGIONS = 128
BUSES = 131072
HOURS = 512


def draw_kkt_inverse(key, part):
    diag_key = jax.random.fold_in(key, 11)
    off_key = jax.random.fold_in(key, 12)
    row_ids = jnp.arange(B)[:, None]
    col_ids = jnp.arange(B)[None, :]
    diagonal = jax.random.uniform(diag_key, (REGIONS, B, 1), jnp.float32, 0.6, 1.4)
    spread = jax.random.normal(off_key, (REGIONS, B, B), jnp.float32) * (0.6 * B ** (-0.5))
    return jnp.where(row_ids == col_ids, diagonal, spread).astype(jnp.bfloat16)


def draw_tie_count(key, part):
    counts = jax.random.randint(jax.random.fold_in(key, 21), (REGIONS,), NS // 4, NS + 1)
    position = jax.random.randint(jax.random.fold_in(key, 22), (), 0, REGIONS)
    return counts.at[position].set(NS).astype(jnp.int32)


def set_ends(values, key, least, top_value):
    longest = values.shape.index(max(values.shape))
    spots = []
    for shift in (0, 1):
        where = [jax.random.randint(jax.random.fold_in(key, axis), (), 0, length) for axis, length in enumerate(values.shape)]
        where[longest] = (where[longest] + shift) % values.shape[longest]
        spots.append(tuple(where))
    return values.at[spots[0]].set(least).at[spots[1]].set(top_value)


def block_scale(rng, dims, cuts, least, high):
    factor_of, own = 1.0, jax.random.fold_in(rng, 6)
    for dim, parts in cuts:
        heights = jnp.exp(jax.random.uniform(jax.random.fold_in(own, dim), (parts,), jnp.float32, least / len(cuts), high / len(cuts)))
        factor_of = factor_of * jnp.repeat(heights, dims[dim] // parts).reshape([-1 if axis == dim else 1 for axis in range(len(dims))])
    return factor_of


def wide_ids(key, extent, number_of, slope):
    portions = [min(1 << octave, number_of + 1 - (1 << octave)) * (1 << 20) // math.isqrt((1 << octave) ** slope) + 1 for octave in range((number_of + 1).bit_length()) if 1 << octave <= number_of]
    scale = 1 + sum(portions) // (1 << 30)
    grid = np.cumsum(np.array([max(1, weight // scale) for weight in portions]))
    lot = jax.random.randint(jax.random.fold_in(key, 1), extent, 0, int(grid[len(portions) - 1]))
    start = jnp.left_shift(1, jnp.searchsorted(jnp.asarray(grid, jnp.int32), lot, side="right").astype(jnp.int32))
    standing = start - 1 + jax.random.randint(jax.random.fold_in(key, 4), extent, 0, 1 << 30) % jnp.minimum(start, number_of + 1 - start)
    return jax.random.permutation(jax.random.fold_in(key, 2), number_of)[standing].astype(jnp.int32)


def bell_draw(key, dims, scale, bound, cuts=(), kind=jnp.bfloat16):
    array = scale * jax.random.normal(key, dims, jnp.float32)
    if cuts:
        array = array * block_scale(key, dims, cuts, -0.22, 0.18)
    return jnp.clip(array, -bound, bound).astype(kind)


def setup_inputs(seed: int = 0) -> dict:
    streams_of = jax.random.split(jax.random.key(seed), 13)
    kkt_inverse = draw_kkt_inverse(jax.random.fold_in(streams_of[12], 71), 0)
    demand = bell_draw(streams_of[1], (HOURS, BUSES), 1.0, 6.0, ((0, 4), (1, 128)), jnp.float32)
    cost_quad = jnp.clip(jnp.exp(math.log(2.0) - 2.9957323 * jax.random.uniform(streams_of[2], (BUSES,), jnp.float32) ** block_scale(streams_of[2], (BUSES,), ((0, 128),), -0.2, 0.2)), 0.1, 2.0)
    cost_lin = jnp.clip(jax.random.uniform(streams_of[3], (BUSES,), jnp.float32, -1.0, 1.0) * block_scale(streams_of[3], (BUSES,), ((0, 128),), -0.4, 0.0), -1.0, 1.0)
    capacity = jnp.clip(jnp.exp(math.log(2.0) - 2.3025851 * jax.random.uniform(streams_of[4], (BUSES,), jnp.float32) ** block_scale(streams_of[4], (BUSES,), ((0, 128),), -0.2, 0.2)), 0.2, 2.0)
    ramp = jnp.clip(jnp.exp(math.log(1.0) - 2.9957323 * jax.random.uniform(streams_of[5], (BUSES,), jnp.float32) ** block_scale(streams_of[5], (BUSES,), ((0, 128),), -0.2, 0.2)), 0.05, 1.0)
    gen_start = jnp.clip(1.0 * jax.random.uniform(streams_of[6], (BUSES,), jnp.float32) ** block_scale(streams_of[6], (BUSES,), ((0, 128),), -0.2, 0.2), 0.0, 1.0)
    boundary_bus = set_ends(jax.random.randint(streams_of[7], (REGIONS, 2, NS), 0, B), jax.random.fold_in(streams_of[7], 1), 0, B - 1).astype(jnp.int32)
    tie_count = draw_tie_count(jax.random.fold_in(streams_of[12], 71), 0)
    part_bus = set_ends(wide_ids(streams_of[9], (PARTS_SIZE, TAPS), BUSES, 2), jax.random.fold_in(streams_of[9], 3), 0, BUSES - 1).astype(jnp.int32)
    part_share = jnp.clip(jnp.exp(jax.random.uniform(streams_of[10], (PARTS_SIZE, TAPS), jnp.float32, math.log(0.05), math.log(1.0))), 0.05, 1.0)
    cleared_mw = bell_draw(streams_of[11], (HOURS // H_DEV, H_DEV, PARTS_SIZE), 1.0, 6.0, ((0, 4), (1, 128)), jnp.float32)
    return dict(kkt_inverse=kkt_inverse, demand=demand, cost_quad=cost_quad, cost_lin=cost_lin, capacity=capacity, ramp=ramp, gen_start=gen_start, boundary_bus=boundary_bus, tie_count=tie_count, part_bus=part_bus, part_share=part_share, cleared_mw=cleared_mw)


def solve_regions(kkt_inverse, right_side):
    hour_count = right_side.shape[0]
    blocks = right_side.reshape(hour_count, REGIONS, B).transpose(1, 0, 2)

    def solve_block(operands):
        matrix, rhs_block = operands
        return jnp.dot(rhs_block.astype(jnp.float32), matrix.astype(jnp.float32).T, preferred_element_type=jnp.float32)

    solved = lax.map(solve_block, (kkt_inverse, blocks))
    return solved.transpose(1, 0, 2).reshape(hour_count, REGIONS * B)


def reference(kkt_inverse, demand, cost_quad, cost_lin, capacity, ramp, gen_start, boundary_bus, tie_count, part_bus, part_share, cleared_mw):
    hour_count = demand.shape[0]
    offsets = (jnp.arange(REGIONS, dtype=jnp.int32) * B)[:, None, None]
    columns = (boundary_bus + offsets).reshape(-1).astype(jnp.int32)
    slot_ids = jnp.arange(NS, dtype=jnp.int32)
    left_live = slot_ids[None, :] < jnp.roll(tie_count, 1)[:, None]
    right_live = slot_ids[None, :] < tie_count[:, None]
    live_mask = jnp.stack([left_live, right_live], axis=1).astype(jnp.float32).reshape(-1)
    generation = jnp.zeros((hour_count, BUSES), jnp.float32)
    dual_var = jnp.zeros((hour_count, BUSES), jnp.float32)
    tie_mean = jnp.zeros((hour_count, REGIONS * 2 * NS), jnp.float32)
    tie_dual = jnp.zeros((hour_count, REGIONS * 2 * NS), jnp.float32)
    angles = generation
    for iteration in range(ITERS):
        tie_term = jnp.zeros((hour_count, BUSES), jnp.float32).at[:, columns].add(live_mask * (tie_mean - tie_dual))
        right_side = (demand + (generation - dual_var) + tie_term).astype(jnp.bfloat16)
        right_side = lax.optimization_barrier(right_side)
        angles = solve_regions(kkt_inverse, right_side)
        at_ends = angles[:, columns]
        tie_ends = at_ends + tie_dual
        shaped = tie_ends.reshape(hour_count, REGIONS, 2, NS)
        far_ends = jnp.stack([jnp.roll(shaped[:, :, 1], 1, axis=1), jnp.roll(shaped[:, :, 0], -1, axis=1)], axis=2).reshape(hour_count, -1)
        tie_mean = live_mask * (tie_ends + far_ends) * 0.5
        tie_dual = live_mask * (tie_dual + at_ends - tie_mean)
        prior_gen = jnp.concatenate([gen_start[None, :], generation[:-1]], axis=0)
        target = (angles + dual_var - cost_lin) / (cost_quad + 1.0)
        limited = jnp.minimum(jnp.maximum(target, prior_gen - ramp), prior_gen + ramp)
        generation = jnp.minimum(jnp.maximum(limited, 0.0), capacity)
        dual_var = dual_var + angles - generation
    prices_bf = dual_var.astype(jnp.bfloat16)
    picked = prices_bf[:, part_bus].astype(jnp.float32)
    prices = jnp.sum(picked * part_share, axis=-1)
    payment = cleared_mw * prices.reshape(cleared_mw.shape)
    return angles, payment
```

```python
import functools

import jax
import jax.numpy as jnp
from jax import lax
from jax.experimental import pallas as pl
from jax.experimental.pallas import tpu as pltpu
from jax.sharding import PartitionSpec as P

MESH = pl.DeviceIdType.MESH
NT = (((1,), (1,)), ((), ()))
LANES = 128


def spread(step, size):
    return (size // 2 + (1 - 2 * (step % 2)) * ((step + 1) // 2)) % size


def kernel(
    torus,
    tie_count,
    kkt_hbm,
    demand_hbm,
    cost_quad,
    cost_lin,
    capacity,
    ramp,
    gen_start,
    boundary,
    part_bus,
    part_share,
    cleared,
    angles_ref,
    payment_ref,
    kkt,
    demand,
    rhs,
    base,
    dual,
    gen,
    slots,
    shares,
    tie_out,
    tie_in,
    edge_out,
    edge_in,
    stage,
    outbox,
    inbox,
    kkt_sem,
    demand_sem,
    tie_send,
    tie_recv,
    edge_send,
    edge_recv,
    price_send,
    price_recv,
):
    size_z, size_y, size_c = torus
    regions = size_z * size_y * size_c
    region = lax.axis_index("region")
    block = lax.axis_index("hour")
    blocks = lax.axis_size("hour")
    right = (region + 1) % regions
    left = (region + regions - 1) % regions
    later = (block + 1) % blocks
    earlier = (block + blocks - 1) % blocks
    hours, buses = demand.shape
    tie_slots = boundary.shape[1]
    chunk = min(256, buses)
    chunks = buses // chunk
    parts = part_bus.shape[1]
    taps = part_bus.shape[0]

    kkt_copies = [
        pltpu.make_async_copy(
            kkt_hbm.at[0, pl.ds(c * chunk, chunk)], kkt.at[pl.ds(c * chunk, chunk)], kkt_sem.at[c]
        )
        for c in range(chunks)
    ]
    demand_copy = pltpu.make_async_copy(demand_hbm, demand, demand_sem)
    demand_copy.start()
    for copy in kkt_copies:
        copy.start()

    barrier = pltpu.get_barrier_semaphore()

    def greet(step, carry):
        pl.semaphore_signal(
            barrier, inc=1, device_id={"region": (region + step) % regions}, device_id_type=MESH
        )
        return carry

    lax.fori_loop(1, regions, greet, 0)
    for neighbour in (earlier, later):
        pl.semaphore_signal(barrier, inc=1, device_id={"hour": neighbour}, device_id_type=MESH)

    lane = lax.broadcasted_iota(jnp.int32, (1, tie_slots), 1)
    row = lax.broadcasted_iota(jnp.int32, (chunk, tie_slots), 0)
    for side, count in ((0, tie_count[left]), (1, tie_count[region])):
        bus = jnp.where(lane < count, boundary[pl.ds(side, 1), :], -1)
        for c in range(chunks):
            slots[pl.ds(c * chunk, chunk), pl.ds(side * tie_slots, tie_slots)] = jnp.where(
                row + c * chunk == bus, 1.0, 0.0
            ).astype(jnp.bfloat16)

    scale = 1.0 / (cost_quad[...] + 1.0)

    demand_copy.wait()
    rhs[...] = demand[...].astype(jnp.bfloat16)

    first_row = lax.broadcasted_iota(jnp.int32, (hours, 1), 0) == 0
    start_row = first_row & (block == 0)
    for c in range(chunks):
        cols = pl.ds(c * chunk, chunk)
        kkt_copies[c].wait()
        angles = lax.dot_general(rhs[...], kkt[cols, :], NT, preferred_element_type=jnp.float32)
        ends = jnp.dot(
            angles.astype(jnp.bfloat16), slots[cols, :], preferred_element_type=jnp.float32
        )
        if c == 0:
            stage_ends = ends
        else:
            stage_ends = stage_ends + ends
        prior = jnp.where(start_row, gen_start[:, cols], 0.0)
        target = (angles - cost_lin[:, cols]) * scale[:, c * chunk : (c + 1) * chunk]
        limited = jnp.minimum(jnp.maximum(target, prior - ramp[:, cols]), prior + ramp[:, cols])
        made = jnp.minimum(jnp.maximum(limited, 0.0), capacity[:, cols])
        owed = angles - made
        gen[:, cols] = made
        dual[:, cols] = owed
        base[:, cols] = demand[:, cols] + (made - owed)
        edge_out[:, cols] = made[hours - 1 :, :]
    for side in range(2):
        tie_out[side] = stage_ends[:, side * tie_slots : (side + 1) * tie_slots].astype(jnp.bfloat16)

    rows = min(64, buses)
    bus_row = lax.broadcasted_iota(jnp.int32, (rows, LANES), 0)

    def fill(step, carry):
        start = step * rows
        for j in range(parts // LANES):
            cols = pl.ds(j * LANES, LANES)
            total = jnp.zeros((rows, LANES), jnp.float32)
            for k in range(taps):
                here = part_bus[pl.ds(k, 1), cols] - (region * buses + start)
                total = total + jnp.where(bus_row == here, part_share[pl.ds(k, 1), cols], 0.0)
            shares[pl.ds(pl.multiple_of(start, rows), rows), cols] = total.astype(jnp.bfloat16)
        return carry

    half = (buses // rows) // 2
    lax.fori_loop(0, half, fill, 0)

    pl.semaphore_wait(barrier, regions + 1)

    ties = [
        pltpu.make_async_remote_copy(
            src_ref=tie_out.at[1 - side],
            dst_ref=tie_in.at[side],
            send_sem=tie_send.at[side],
            recv_sem=tie_recv.at[side],
            device_id={"region": to},
            device_id_type=MESH,
        )
        for side, to in ((0, right), (1, left))
    ]
    edge = pltpu.make_async_remote_copy(
        src_ref=edge_out,
        dst_ref=edge_in,
        send_sem=edge_send,
        recv_sem=edge_recv,
        device_id={"hour": later},
        device_id_type=MESH,
    )
    for copy in ties:
        copy.start()
    edge.start()

    lax.fori_loop(half, buses // rows, fill, 0)

    for copy in ties:
        copy.wait()
    edge.wait()

    for c in range(chunks):
        cols = pl.ds(c * chunk, chunk)
        tied = base[:, cols]
        for side in range(2):
            tied = tied + lax.dot_general(
                tie_in[side],
                slots[cols, pl.ds(side * tie_slots, tie_slots)],
                NT,
                preferred_element_type=jnp.float32,
            )
        rhs[:, cols] = tied.astype(jnp.bfloat16)

    for c in range(chunks):
        cols = pl.ds(c * chunk, chunk)
        angles = lax.dot_general(rhs[...], kkt[cols, :], NT, preferred_element_type=jnp.float32)
        angles_ref[:, cols] = angles
        before = jnp.where(block == 0, gen_start[:, cols], edge_in[:, cols])
        prior = jnp.where(first_row, before, pltpu.roll(gen[:, cols], 1, 0))
        owed = dual[:, cols]
        target = (angles + owed - cost_lin[:, cols]) * scale[:, c * chunk : (c + 1) * chunk]
        limited = jnp.minimum(jnp.maximum(target, prior - ramp[:, cols]), prior + ramp[:, cols])
        made = jnp.minimum(jnp.maximum(limited, 0.0), capacity[:, cols])
        base[:, cols] = owed + angles - made

    lmp = base[...].astype(jnp.bfloat16)
    pieces = parts // LANES
    width = min(256, parts)
    for c in range(parts // width):
        part = jnp.dot(lmp, shares[:, pl.ds(c * width, width)], preferred_element_type=jnp.float32)
        for i in range(width // LANES):
            stage[pl.ds(c * (width // LANES) + i, hours, stride=pieces), :] = part[
                :, i * LANES : (i + 1) * LANES
            ]
    outbox[...] = stage[...].reshape(hours, pieces, LANES).astype(jnp.bfloat16)

    here_z = region // (size_y * size_c)
    here_y = (region // size_c) % size_y
    here_c = region % size_c

    def send(to):
        pltpu.make_async_remote_copy(
            src_ref=outbox.at[to],
            dst_ref=inbox.at[region],
            send_sem=price_send,
            recv_sem=price_recv,
            device_id={"region": to},
            device_id_type=MESH,
        ).start()

    def post(step, carry):
        to_z = (here_z + spread(step // size_y, size_z)) % size_z
        to_y = (here_y + spread(step % size_y, size_y)) % size_y
        for shift in range(size_c):
            send((to_z * size_y + to_y) * size_c + (here_c + shift) % size_c)
        return carry

    lax.fori_loop(0, size_z * size_y - 1, post, 0)
    for shift in range(1, size_c):
        send((here_z * size_y + here_y) * size_c + (here_c + shift) % size_c)
    inbox[region] = outbox[region]

    others = pl.ds(0, regions - 1)
    whole = pltpu.make_async_remote_copy(
        src_ref=outbox.at[others],
        dst_ref=inbox.at[others],
        send_sem=price_send,
        recv_sem=price_recv,
        device_id={"region": right},
        device_id_type=MESH,
    )
    whole.wait_recv()
    price = jnp.sum(inbox[...].astype(jnp.float32), axis=0)
    payment_ref[...] = cleared[...] * price
    whole.wait_send()


def settle(torus, *operands):
    (
        kkt_inverse,
        demand,
        cost_quad,
        cost_lin,
        capacity,
        ramp,
        gen_start,
        boundary_bus,
        tie_count,
        part_bus,
        part_share,
        cleared_mw,
    ) = operands
    hours, buses = demand.shape
    tie_slots = boundary_bus.shape[2]
    parts = part_bus.shape[0]
    pieces = parts // LANES
    regions = torus[0] * torus[1] * torus[2]
    chunks = max(1, buses // 256)
    line = lambda value: value.reshape(1, buses)
    vmem = pl.BlockSpec(memory_space=pltpu.VMEM)
    hbm = pl.BlockSpec(memory_space=pl.ANY)
    bf16, f32 = jnp.bfloat16, jnp.float32
    angles, payment = pl.pallas_call(
        functools.partial(kernel, torus),
        out_shape=(
            jax.ShapeDtypeStruct((hours, buses), f32),
            jax.ShapeDtypeStruct((pieces, LANES), f32),
        ),
        in_specs=[pl.BlockSpec(memory_space=pltpu.SMEM), hbm, hbm] + [vmem] * 9,
        out_specs=(vmem, vmem),
        scratch_shapes=[
            pltpu.VMEM((buses, buses), bf16),
            pltpu.VMEM((hours, buses), f32),
            pltpu.VMEM((hours, buses), bf16),
            pltpu.VMEM((hours, buses), f32),
            pltpu.VMEM((hours, buses), f32),
            pltpu.VMEM((hours, buses), f32),
            pltpu.VMEM((buses, 2 * tie_slots), bf16),
            pltpu.VMEM((buses, parts), bf16),
            pltpu.VMEM((2, hours, tie_slots), bf16),
            pltpu.VMEM((2, hours, tie_slots), bf16),
            pltpu.VMEM((1, buses), f32),
            pltpu.VMEM((1, buses), f32),
            pltpu.VMEM((hours * pieces, LANES), f32),
            pltpu.VMEM((regions, pieces, LANES), bf16),
            pltpu.VMEM((regions, pieces, LANES), bf16),
            pltpu.SemaphoreType.DMA((chunks,)),
            pltpu.SemaphoreType.DMA,
            pltpu.SemaphoreType.DMA((2,)),
            pltpu.SemaphoreType.DMA((2,)),
            pltpu.SemaphoreType.DMA,
            pltpu.SemaphoreType.DMA,
            pltpu.SemaphoreType.DMA,
            pltpu.SemaphoreType.DMA,
        ],
        compiler_params=pltpu.CompilerParams(collective_id=0, has_side_effects=True),
    )(
        tie_count,
        kkt_inverse,
        demand,
        line(cost_quad),
        line(cost_lin),
        line(capacity),
        line(ramp),
        line(gen_start),
        boundary_bus[0],
        part_bus.T,
        part_share.T,
        cleared_mw.reshape(pieces, LANES),
    )
    return angles, payment.reshape(cleared_mw.shape)


def solution(mesh, torus=(8, 8, 2)):
    return jax.shard_map(
        functools.partial(settle, torus),
        mesh=mesh,
        in_specs=(
            P("region", None, None),
            P("hour", "region"),
            P("region"),
            P("region"),
            P("region"),
            P("region"),
            P("region"),
            P("region", None, None),
            P(),
            P(),
            P(),
            P("hour", "region", None),
        ),
        out_specs=(P("hour", "region"), P("hour", "region", None)),
        check_vma=False,
    )
```

```python
import functools

import jax
import jax.numpy as jnp
from jax import lax
from jax.experimental import pallas as pl
from jax.experimental.pallas import tpu as pltpu
from jax.sharding import PartitionSpec as P

MESH = pl.DeviceIdType.MESH
NT = (((1,), (1,)), ((), ()))
LANES = 128
PAD = 8


def far_first(size):
    return sorted(range(1, size), key=lambda shift: -min(shift, size - shift))


def kernel(
    torus,
    boundary_hbm,
    tie_count_hbm,
    demand_hbm,
    kkt_hbm,
    cost_quad_hbm,
    cost_lin_hbm,
    capacity_hbm,
    ramp_hbm,
    gen_start_hbm,
    part_bus_hbm,
    part_share_hbm,
    angles_ref,
    price_ref,
    boundary,
    tie_count,
    demand,
    kkt,
    cost_quad,
    cost_lin,
    capacity,
    ramp,
    gen_start,
    part_bus,
    part_share,
    rhs,
    lmp,
    base,
    dual,
    gen,
    slots,
    spread,
    shares,
    tie_out,
    tie_in,
    edge_out,
    edge_in,
    stage,
    out_y,
    out_z,
    in_y,
    in_z,
    out_last,
    in_last,
    load_sem,
    kkt_sem,
    tie_send,
    tie_recv,
    edge_sem,
    ring_send,
    ring_recv,
    last_sem,
):
    size_z, size_y, size_c = torus
    regions = size_z * size_y * size_c
    region = lax.axis_index("region")
    block = lax.axis_index("hour")
    blocks = lax.axis_size("hour")
    z = region // (size_y * size_c)
    y = (region // size_c) % size_y
    core = region % size_c
    right = (region + 1) % regions
    left = (region + regions - 1) % regions
    later = (block + 1) % blocks
    earlier = (block + blocks - 1) % blocks
    hours, buses = demand.shape
    tie_slots = boundary.shape[1]
    chunk = min(256, buses)
    chunks = buses // chunk
    taps, parts = part_bus.shape
    pieces = parts // LANES
    f32, bf16 = jnp.float32, jnp.bfloat16

    def at(to_z, to_y, to_c):
        return {"region": (to_z * size_y + to_y) * size_c + to_c}

    def load(index, source, target):
        copy = pltpu.make_async_copy(source, target, load_sem.at[index])
        copy.start()
        return copy

    def send(source, target, sems, to):
        copy = pltpu.make_async_remote_copy(
            src_ref=source,
            dst_ref=target,
            send_sem=sems[0],
            recv_sem=sems[1],
            device_id=to,
            device_id_type=MESH,
        )
        copy.start()
        return copy

    slot_loads = [load(0, boundary_hbm, boundary), load(1, tie_count_hbm, tie_count)]
    demand_load = load(2, demand_hbm, demand)
    kkt_loads = []
    for c in range(chunks):
        copy = pltpu.make_async_copy(
            kkt_hbm.at[0, pl.ds(c * chunk, chunk)], kkt.at[pl.ds(c * chunk, chunk)], kkt_sem.at[c]
        )
        copy.start()
        kkt_loads.append(copy)
    cost_loads = [
        load(3, cost_quad_hbm, cost_quad),
        load(4, cost_lin_hbm, cost_lin),
        load(5, capacity_hbm, capacity),
        load(6, ramp_hbm, ramp),
        load(7, gen_start_hbm, gen_start),
    ]
    part_loads = [load(8, part_bus_hbm, part_bus), load(9, part_share_hbm, part_share)]

    barrier = pltpu.get_barrier_semaphore()
    shifts_y = far_first(size_y)
    shifts_z = far_first(size_z)
    greeted = 0

    def greet(to):
        pl.semaphore_signal(barrier, inc=1, device_id=to, device_id_type=MESH)
        return 1

    for shift in shifts_y:
        for other in range(size_c):
            greeted += greet(at(z, (y + shift) % size_y, (core + other) % size_c))
    for shift in shifts_z:
        for other in range(size_c):
            greeted += greet(at((z + shift) % size_z, y, (core + other) % size_c))
    greeted += greet(at(z, y, 1 - core))
    for neighbour in (right, left):
        greeted += greet({"region": neighbour})
    for neighbour in (earlier, later):
        greeted += greet({"hour": neighbour})

    for copy in slot_loads:
        copy.wait()
    lane = lax.broadcasted_iota(jnp.int32, (1, tie_slots), 1)
    owner = lax.broadcasted_iota(jnp.int32, (1, regions), 1)
    row = lax.broadcasted_iota(jnp.int32, (chunk, tie_slots), 0)
    for side, edge_region in ((0, left), (1, region)):
        count = jnp.sum(
            jnp.where(owner == edge_region, tie_count[...], 0), axis=1, keepdims=True
        )
        bus = jnp.where(lane < count, boundary[pl.ds(side, 1), :], -1)
        for c in range(chunks):
            slots[pl.ds(c * chunk, chunk), pl.ds(side * tie_slots, tie_slots)] = jnp.where(
                row + c * chunk == bus, 1.0, 0.0
            ).astype(bf16)

    demand_load.wait()
    rhs[...] = demand[...].astype(bf16)
    for c in range(chunks):
        cols = pl.ds(c * chunk, chunk)
        kkt_loads[c].wait()
        angles = lax.dot_general(rhs[...], kkt[cols, :], NT, preferred_element_type=f32)
        angles_ref[:, cols] = angles
        part = jnp.dot(angles.astype(bf16), slots[cols, :], preferred_element_type=f32)
        ends = part if c == 0 else ends + part
    for side in range(2):
        tie_out[side] = ends[:, side * tie_slots : (side + 1) * tie_slots].astype(bf16)

    pl.semaphore_wait(barrier, greeted)
    ties = [
        send(tie_out.at[1 - side], tie_in.at[side], (tie_send.at[side], tie_recv.at[side]), to)
        for side, to in ((0, {"region": right}), (1, {"region": left}))
    ]

    for copy in cost_loads:
        copy.wait()
    tall = min(32, hours)
    start_row = (lax.broadcasted_iota(jnp.int32, (tall, chunk), 0) == 0) & (block == 0)
    for c in range(chunks):
        cols = pl.ds(c * chunk, chunk)
        scale = 1.0 / (cost_quad[:, cols] + 1.0)
        for r in range(hours // tall):
            rows = pl.ds(r * tall, tall)
            angles = angles_ref[rows, cols]
            target = (angles - cost_lin[:, cols]) * scale
            if r == 0:
                prior = jnp.where(start_row, gen_start[:, cols], 0.0)
                limited = jnp.minimum(
                    jnp.maximum(target, prior - ramp[:, cols]), prior + ramp[:, cols]
                )
            else:
                limited = jnp.minimum(jnp.maximum(target, -ramp[:, cols]), ramp[:, cols])
            made = jnp.minimum(jnp.maximum(limited, 0.0), capacity[:, cols])
            owed = angles - made
            gen[pl.ds(PAD + r * tall, tall), cols] = made
            dual[rows, cols] = owed
            base[rows, cols] = demand[rows, cols] + (made - owed)
        edge_out[:, cols] = made[tall - 1 :, :]
    edge = send(edge_out, edge_in, (edge_sem.at[0], edge_sem.at[1]), {"hour": later})

    for copy in part_loads:
        copy.wait()
    high = buses // LANES
    tile = lax.broadcasted_iota(jnp.int32, (16, LANES), 0)

    def fill(step, carry):
        cols = pl.ds(pl.multiple_of(step * LANES, LANES), LANES)
        low = []
        for k in range(taps):
            local = part_bus[pl.ds(k, 1), cols] - region * buses
            share = part_share[pl.ds(k, 1), cols]
            low.append(jnp.broadcast_to(local & (LANES - 1), (16, LANES)))
            for i in range(high):
                held = jnp.where((local >> 7) == i, share, 0.0)
                spread[k * high + i] = jnp.broadcast_to(held, (16, LANES)).astype(bf16)
        for t in range(LANES // 16):
            ones = [jnp.where(tile + 16 * t == low[k], 1.0, 0.0).astype(bf16) for k in range(taps)]
            for i in range(high):
                total = ones[0] * spread[i]
                for k in range(1, taps):
                    total = total + ones[k] * spread[k * high + i]
                shares[pl.ds(i * LANES + t * 16, 16), cols] = total
        return carry

    lax.fori_loop(0, pieces, fill, 0)

    for copy in ties:
        copy.wait()
    for c in range(chunks):
        cols = pl.ds(c * chunk, chunk)
        tied = base[:, cols]
        for side in range(2):
            tied = tied + lax.dot_general(
                tie_in[side],
                slots[cols, pl.ds(side * tie_slots, tie_slots)],
                NT,
                preferred_element_type=f32,
            )
        rhs[:, cols] = tied.astype(bf16)

    edge.wait()
    gen[pl.ds(PAD - 1, 1), :] = jnp.where(block == 0, gen_start[...], edge_in[...])
    for c in range(chunks):
        cols = pl.ds(c * chunk, chunk)
        angles_ref[:, cols] = lax.dot_general(
            rhs[...], kkt[cols, :], NT, preferred_element_type=f32
        )
    for c in range(chunks):
        cols = pl.ds(c * chunk, chunk)
        scale = 1.0 / (cost_quad[:, cols] + 1.0)
        for r in range(hours // tall):
            rows = pl.ds(r * tall, tall)
            owed = dual[rows, cols] + angles_ref[rows, cols]
            prior = gen[pl.ds(PAD - 1 + r * tall, tall), cols]
            target = (owed - cost_lin[:, cols]) * scale
            limited = jnp.minimum(
                jnp.maximum(target, prior - ramp[:, cols]), prior + ramp[:, cols]
            )
            made = jnp.minimum(jnp.maximum(limited, 0.0), capacity[:, cols])
            lmp[rows, cols] = (owed - made).astype(bf16)

    width = min(256, parts)
    for c in range(parts // width):
        part = jnp.dot(lmp[...], shares[:, pl.ds(c * width, width)], preferred_element_type=f32)
        for i in range(width // LANES):
            stage[pl.ds(c * (width // LANES) + i, hours, stride=pieces), :] = part[
                :, i * LANES : (i + 1) * LANES
            ]
    for hour in range(hours):
        to_z, to_y, to_c = hour // (size_y * size_c), (hour // size_c) % size_y, hour % size_c
        row_price = stage[pl.ds(hour * pieces, pieces), :].astype(bf16)
        if to_c == 0:
            out_y[to_y, to_z] = row_price
        else:
            out_z[to_z, to_y] = row_price

    sems_y = (ring_send.at[0], ring_recv.at[0])
    sems_z = (ring_send.at[1], ring_recv.at[1])
    for shift_y, shift_z in zip(shifts_y, shifts_z):
        to_y, to_z = (y + shift_y) % size_y, (z + shift_z) % size_z
        send(out_y.at[to_y], in_y.at[y], sems_y, at(z, to_y, core))
        send(out_z.at[to_z], in_z.at[z], sems_z, at(to_z, y, core))

    def whole(source, target, count, sems):
        some = pl.ds(0, count)
        return pltpu.make_async_remote_copy(
            src_ref=source.at[some],
            dst_ref=target.at[some],
            send_sem=sems[0],
            recv_sem=sems[1],
            device_id={"region": right},
            device_id_type=MESH,
        )

    all_y = whole(out_y, in_y, size_y - 1, sems_y)
    all_z = whole(out_z, in_z, size_z - 1, sems_z)
    all_y.wait_recv()
    total = out_y[y].astype(f32)
    for shift in range(1, size_y):
        total = total + in_y[(y + shift) % size_y].astype(f32)
    out_last[pl.ds(0, size_z)] = total
    sems_last = (last_sem.at[0], last_sem.at[1])
    for shift in shifts_z:
        to_z = (z + shift) % size_z
        send(out_last.at[to_z], in_last.at[z * size_c + core], sems_last, at(to_z, y, 0))
    all_z.wait_recv()
    total = out_z[z].astype(f32)
    for shift in range(1, size_z):
        total = total + in_z[(z + shift) % size_z].astype(f32)
    out_last[pl.ds(size_z, size_y)] = total
    for shift in shifts_y:
        to_y = (y + shift) % size_y
        send(out_last.at[size_z + to_y], in_last.at[y * size_c + core], sems_last, at(z, to_y, 1))
    theirs = (1 - core) * (size_z + y) + core * z
    send(
        out_last.at[theirs],
        in_last.at[(1 - core) * y * size_c + core * (z * size_c + 1)],
        sems_last,
        at(z, y, 1 - core),
    )
    mine = (1 - core) * z + core * (size_z + y)
    slot = (1 - core) * z * size_c + core * (y * size_c + 1)
    sources = size_z * size_c
    all_last = whole(out_last, in_last, sources - 1, sems_last)
    all_y.wait_send()
    all_z.wait_send()
    all_last.wait_recv()
    price = out_last[mine]
    for shift in range(1, sources):
        price = price + in_last[(slot + shift) % sources]
    price_ref[...] = price
    all_last.wait_send()


def finish(angles, price, cleared, angles_hbm, payment, sem):
    copy = pltpu.make_async_copy(angles, angles_hbm, sem)
    copy.start()
    payment[...] = cleared[...] * price[...]
    copy.wait()


def settle(torus, *operands):
    (
        kkt_inverse,
        demand,
        cost_quad,
        cost_lin,
        capacity,
        ramp,
        gen_start,
        boundary_bus,
        tie_count,
        part_bus,
        part_share,
        cleared_mw,
    ) = operands
    hours, buses = demand.shape
    tie_slots = boundary_bus.shape[2]
    parts, taps = part_share.shape
    pieces = parts // LANES
    size_z, size_y, size_c = torus
    chunks = max(1, buses // 256)
    line = lambda value: value.reshape(1, -1)
    vmem = pl.BlockSpec(memory_space=pltpu.VMEM)
    hbm = pl.BlockSpec(memory_space=pltpu.HBM)
    bf16, f32, i32 = jnp.bfloat16, jnp.float32, jnp.int32
    dma = pltpu.SemaphoreType.DMA
    angles, price = pl.pallas_call(
        functools.partial(kernel, torus),
        out_shape=(
            jax.ShapeDtypeStruct((hours, buses), f32),
            jax.ShapeDtypeStruct((pieces, LANES), f32),
        ),
        in_specs=[hbm] * 11,
        out_specs=(vmem, vmem),
        scratch_shapes=[
            pltpu.VMEM((2, tie_slots), i32),
            pltpu.VMEM((1, tie_count.shape[0]), i32),
            pltpu.VMEM((hours, buses), f32),
            pltpu.VMEM((buses, buses), bf16),
            pltpu.VMEM((1, buses), f32),
            pltpu.VMEM((1, buses), f32),
            pltpu.VMEM((1, buses), f32),
            pltpu.VMEM((1, buses), f32),
            pltpu.VMEM((1, buses), f32),
            pltpu.VMEM((taps, parts), i32),
            pltpu.VMEM((taps, parts), f32),
            pltpu.VMEM((hours, buses), bf16),
            pltpu.VMEM((hours, buses), bf16),
            pltpu.VMEM((hours, buses), f32),
            pltpu.VMEM((hours, buses), f32),
            pltpu.VMEM((PAD + hours, buses), f32),
            pltpu.VMEM((buses, 2 * tie_slots), bf16),
            pltpu.VMEM((taps * (buses // LANES), 16, LANES), bf16),
            pltpu.VMEM((buses, parts), bf16),
            pltpu.VMEM((2, hours, tie_slots), bf16),
            pltpu.VMEM((2, hours, tie_slots), bf16),
            pltpu.VMEM((1, buses), f32),
            pltpu.VMEM((1, buses), f32),
            pltpu.VMEM((hours * pieces, LANES), f32),
            pltpu.VMEM((size_y, size_z, pieces, LANES), bf16),
            pltpu.VMEM((size_z, size_y, pieces, LANES), bf16),
            pltpu.VMEM((size_y, size_z, pieces, LANES), bf16),
            pltpu.VMEM((size_z, size_y, pieces, LANES), bf16),
            pltpu.VMEM((size_z + size_y, pieces, LANES), f32),
            pltpu.VMEM((size_z * size_c, pieces, LANES), f32),
            dma((10,)),
            dma((chunks,)),
            dma((2,)),
            dma((2,)),
            dma((2,)),
            dma((2,)),
            dma((2,)),
            dma((2,)),
        ],
        compiler_params=pltpu.CompilerParams(
            collective_id=0, has_side_effects=True, vmem_limit_bytes=16 * 1024 * 1024
        ),
    )(*[pltpu.with_memory_space_constraint(v, pltpu.HBM) for v in (
        boundary_bus[0],
        line(tie_count),
        demand,
        kkt_inverse,
        line(cost_quad),
        line(cost_lin),
        line(capacity),
        line(ramp),
        line(gen_start),
        part_bus.T,
        part_share.T,
    )])
    angles, payment = pl.pallas_call(
        finish,
        out_shape=(
            jax.ShapeDtypeStruct((hours, buses), f32),
            jax.ShapeDtypeStruct((pieces, LANES), f32),
        ),
        in_specs=[vmem] * 3,
        out_specs=(pl.BlockSpec(memory_space=pl.ANY), vmem),
        scratch_shapes=[dma],
        compiler_params=pltpu.CompilerParams(vmem_limit_bytes=16 * 1024 * 1024),
    )(angles, price, cleared_mw.reshape(pieces, LANES))
    return angles, payment.reshape(cleared_mw.shape)


def solution(mesh, torus=(8, 8, 2)):
    return jax.shard_map(
        functools.partial(settle, torus),
        mesh=mesh,
        in_specs=(
            P("region", None, None),
            P("hour", "region"),
            P("region"),
            P("region"),
            P("region"),
            P("region"),
            P("region"),
            P("region", None, None),
            P(),
            P(),
            P(),
            P("hour", "region", None),
        ),
        out_specs=(P("hour", "region"), P("hour", "region", None)),
        check_vma=False,
    )
```

```python
import functools

import jax
import jax.numpy as jnp
from jax import lax
from jax.experimental import pallas as pl
from jax.experimental.pallas import tpu as pltpu
from jax.sharding import PartitionSpec as P

MESH = pl.DeviceIdType.MESH
NT = (((1,), (1,)), ((), ()))
LANES = 128
PAD = 8


def far_first(size):
    return sorted(range(1, size), key=lambda shift: -min(shift, size - shift))


def far_first_all(torus):
    size_z, size_y, _ = torus
    shifts = [(a, b) for a in range(size_z) for b in range(size_y)]
    hops = lambda shift: min(shift[0], size_z - shift[0]) + min(shift[1], size_y - shift[1])
    return sorted(shifts[1:], key=lambda shift: -hops(shift))


def kernel(
    torus,
    boundary_hbm,
    tie_count_hbm,
    demand_hbm,
    kkt_hbm,
    cost_quad_hbm,
    cost_lin_hbm,
    capacity_hbm,
    ramp_hbm,
    gen_start_hbm,
    part_bus_hbm,
    part_share_hbm,
    angles_ref,
    price_ref,
    boundary,
    tie_count,
    demand,
    kkt,
    cost_quad,
    cost_lin,
    capacity,
    ramp,
    gen_start,
    part_bus,
    part_share,
    rhs,
    lmp,
    base,
    dual,
    gen,
    low_bound,
    high_bound,
    scale,
    slots,
    spread,
    shares,
    tie_out,
    tie_in,
    edge_out,
    edge_in,
    stage,
    pair_out,
    pair_in,
    outbox,
    inbox,
    load_sem,
    kkt_sem,
    tie_send,
    tie_recv,
    edge_sem,
    known,
    pair_sem,
    price_sem,
):
    size_z, size_y, size_c = torus
    regions = size_z * size_y * size_c
    region = lax.axis_index("region")
    block = lax.axis_index("hour")
    blocks = lax.axis_size("hour")
    z = region // (size_y * size_c)
    y = (region // size_c) % size_y
    core = region % size_c
    right = (region + 1) % regions
    left = (region + regions - 1) % regions
    later = (block + 1) % blocks
    earlier = (block + blocks - 1) % blocks
    hours, buses = demand.shape
    tie_slots = boundary.shape[1]
    chunk = min(256, buses)
    chunks = buses // chunk
    taps, parts = part_bus.shape
    pieces = parts // LANES
    f32, bf16 = jnp.float32, jnp.bfloat16

    def at(to_z, to_y, to_c):
        return {"region": (to_z * size_y + to_y) * size_c + to_c}

    def load(index, source, target):
        copy = pltpu.make_async_copy(source, target, load_sem.at[index])
        copy.start()
        return copy

    def send(source, target, sems, to):
        copy = pltpu.make_async_remote_copy(
            src_ref=source,
            dst_ref=target,
            send_sem=sems[0],
            recv_sem=sems[1],
            device_id=to,
            device_id_type=MESH,
        )
        copy.start()
        return copy

    slot_loads = [load(0, boundary_hbm, boundary), load(1, tie_count_hbm, tie_count)]
    demand_load = load(2, demand_hbm, demand)
    kkt_loads = []
    for c in range(chunks):
        copy = pltpu.make_async_copy(
            kkt_hbm.at[0, pl.ds(c * chunk, chunk)], kkt.at[pl.ds(c * chunk, chunk)], kkt_sem.at[c]
        )
        copy.start()
        kkt_loads.append(copy)
    pair_of = min(2, chunks)
    cost_loads = [
        load(3, cost_quad_hbm, cost_quad),
        load(4, cost_lin_hbm, cost_lin),
        load(5, capacity_hbm, capacity),
        load(6, ramp_hbm, ramp),
        load(7, gen_start_hbm, gen_start),
    ]
    part_loads = [load(8, part_bus_hbm, part_bus), load(9, part_share_hbm, part_share)]

    barrier = pltpu.get_barrier_semaphore()
    shifts_y = far_first(size_y)
    shifts_z = far_first(size_z)
    greeted = 0

    def greet(to):
        pl.semaphore_signal(barrier, inc=1, device_id=to, device_id_type=MESH)
        return 1

    for shift in shifts_y:
        for other in range(size_c):
            greeted += greet(at(z, (y + shift) % size_y, (core + other) % size_c))
    for shift in shifts_z:
        for other in range(size_c):
            greeted += greet(at((z + shift) % size_z, y, (core + other) % size_c))
    greeted += greet(at(z, y, 1 - core))
    for neighbour in (right, left):
        greeted += greet({"region": neighbour})
    for neighbour in (earlier, later):
        greeted += greet({"hour": neighbour})

    for copy in slot_loads:
        copy.wait()
    lane = lax.broadcasted_iota(jnp.int32, (1, tie_slots), 1)
    owner = lax.broadcasted_iota(jnp.int32, (1, regions), 1)
    row = lax.broadcasted_iota(jnp.int32, (chunk, tie_slots), 0)
    for side, edge_region in ((0, left), (1, region)):
        count = jnp.sum(
            jnp.where(owner == edge_region, tie_count[...], 0), axis=1, keepdims=True
        )
        bus = jnp.where(lane < count, boundary[pl.ds(side, 1), :], -1)
        for c in range(chunks):
            slots[pl.ds(c * chunk, chunk), pl.ds(side * tie_slots, tie_slots)] = jnp.where(
                row + c * chunk == bus, 1.0, 0.0
            ).astype(bf16)

    demand_load.wait()
    rhs[...] = demand[...].astype(bf16)
    for first in range(0, chunks, pair_of):
        for c in range(first, first + pair_of):
            kkt_loads[c].wait()
        both = [
            lax.dot_general(
                rhs[...], kkt[pl.ds(c * chunk, chunk), :], NT, preferred_element_type=f32
            )
            for c in range(first, first + pair_of)
        ]
        for c, angles in enumerate(both, first):
            angles_ref[:, pl.ds(c * chunk, chunk)] = angles
            part = jnp.dot(
                angles.astype(bf16),
                slots[pl.ds(c * chunk, chunk), :],
                preferred_element_type=f32,
            )
            ends = part if c == 0 else ends + part
    for side in range(2):
        tie_out[side] = ends[:, side * tie_slots : (side + 1) * tie_slots].astype(bf16)

    pl.semaphore_wait(barrier, greeted)
    for shift in shifts_y:
        pl.semaphore_signal(
            known, inc=1, device_id=at(z, (y + shift) % size_y, core), device_id_type=MESH
        )
    ties = [
        send(tie_out.at[1 - side], tie_in.at[side], (tie_send.at[side], tie_recv.at[side]), to)
        for side, to in ((0, {"region": right}), (1, {"region": left}))
    ]

    for copy in cost_loads:
        copy.wait()
    tall = min(32, hours)
    start_row = (lax.broadcasted_iota(jnp.int32, (tall, chunk), 0) == 0) & (block == 0)
    for c in range(chunks):
        cols = pl.ds(c * chunk, chunk)
        scale[:, cols] = 1.0 / (cost_quad[:, cols] + 1.0)
        for r in range(hours // tall):
            rows = pl.ds(r * tall, tall)
            angles = angles_ref[rows, cols]
            target = (angles - cost_lin[:, cols]) * scale[:, cols]
            if r == 0:
                prior = jnp.where(start_row, gen_start[:, cols], 0.0)
                limited = jnp.minimum(
                    jnp.maximum(target, prior - ramp[:, cols]), prior + ramp[:, cols]
                )
            else:
                limited = jnp.minimum(jnp.maximum(target, -ramp[:, cols]), ramp[:, cols])
            made = jnp.minimum(jnp.maximum(limited, 0.0), capacity[:, cols])
            owed = angles - made
            gen[pl.ds(PAD + r * tall, tall), cols] = made
            dual[rows, cols] = owed
            base[rows, cols] = demand[rows, cols] + (made - owed)
        edge_out[:, cols] = made[tall - 1 :, :]
        for r in range(hours // tall):
            rows = pl.ds(r * tall, tall)
            prior = gen[pl.ds(PAD - 1 + r * tall, tall), cols]
            top = capacity[:, cols]
            low_bound[rows, cols] = jnp.minimum(jnp.maximum(prior - ramp[:, cols], 0.0), top)
            high_bound[rows, cols] = jnp.minimum(jnp.maximum(prior + ramp[:, cols], 0.0), top)
    edge = send(edge_out, edge_in, (edge_sem.at[0], edge_sem.at[1]), {"hour": later})

    for copy in part_loads:
        copy.wait()
    high = buses // LANES
    tile = lax.broadcasted_iota(jnp.int32, (16, LANES), 0).astype(f32).astype(bf16)
    one, zero = jnp.ones((16, LANES), bf16), jnp.zeros((16, LANES), bf16)

    def fill(step, carry):
        cols = pl.ds(pl.multiple_of(step * LANES, LANES), LANES)
        low = []
        for k in range(taps):
            local = part_bus[pl.ds(k, 1), cols] - region * buses
            share = part_share[pl.ds(k, 1), cols]
            place = (local & (LANES - 1)).astype(f32)
            low.append(jnp.broadcast_to(place, (16, LANES)).astype(bf16))
            for i in range(high):
                held = jnp.where((local >> 7) == i, share, 0.0)
                spread[k * high + i] = jnp.broadcast_to(held, (16, LANES)).astype(bf16)
        for t in range(LANES // 16):
            place = tile + jnp.bfloat16(16 * t)
            ones = [jnp.where(place == low[k], one, zero) for k in range(taps)]
            for i in range(high):
                total = ones[0] * spread[i]
                for k in range(1, taps):
                    total = total + ones[k] * spread[k * high + i]
                shares[pl.ds(i * LANES + t * 16, 16), cols] = total
        return carry

    lax.fori_loop(0, pieces, fill, 0)

    for copy in ties:
        copy.wait()
    for c in range(chunks):
        cols = pl.ds(c * chunk, chunk)
        tied = base[:, cols]
        for side in range(2):
            tied = tied + lax.dot_general(
                tie_in[side],
                slots[cols, pl.ds(side * tie_slots, tie_slots)],
                NT,
                preferred_element_type=f32,
            )
        rhs[:, cols] = tied.astype(bf16)

    edge.wait()
    prior = jnp.where(block == 0, gen_start[...], edge_in[...])
    low_bound[pl.ds(0, 1), :] = jnp.minimum(jnp.maximum(prior - ramp[...], 0.0), capacity[...])
    high_bound[pl.ds(0, 1), :] = jnp.minimum(jnp.maximum(prior + ramp[...], 0.0), capacity[...])
    for first in range(0, chunks, pair_of):
        for c in range(first, first + pair_of):
            cols = pl.ds(c * chunk, chunk)
            angles_ref[:, cols] = lax.dot_general(
                rhs[...], kkt[cols, :], NT, preferred_element_type=f32
            )
    for c in range(chunks):
        cols = pl.ds(c * chunk, chunk)
        for r in range(hours // tall):
            rows = pl.ds(r * tall, tall)
            owed = dual[rows, cols] + angles_ref[rows, cols]
            target = (owed - cost_lin[:, cols]) * scale[:, cols]
            made = jnp.minimum(jnp.maximum(target, low_bound[rows, cols]), high_bound[rows, cols])
            lmp[rows, cols] = (owed - made).astype(bf16)

    width = min(256, parts)
    for c in range(parts // width):
        part = jnp.dot(lmp[...], shares[:, pl.ds(c * width, width)], preferred_element_type=f32)
        for i in range(width // LANES):
            stage[pl.ds(c * (width // LANES) + i, hours, stride=pieces), :] = part[
                :, i * LANES : (i + 1) * LANES
            ]
    chips = size_z * size_y

    def priced(chip, owner):
        return stage[pl.ds(pl.multiple_of((chip * size_c + owner) * pieces, pieces), pieces), :]

    for chip in range(chips):
        pair_out[chip] = priced(chip, 1 - core).astype(bf16)
    pair = send(pair_out, pair_in, (pair_sem.at[0], pair_sem.at[1]), at(z, y, 1 - core))
    to_zs = [(z + shift) % size_z * size_y for shift in range(size_z)]
    to_ys = [(y + shift) % size_y for shift in range(size_y)]
    pl.semaphore_wait(known, size_y - 1)
    pair.wait()
    for chip in range(chips):
        outbox[chip] = (priced(chip, core) + pair_in[chip].astype(f32)).astype(bf16)

    here = z * size_y + y
    sems = (price_sem.at[0], price_sem.at[1])
    for shift_z, shift_y in far_first_all(torus):
        chip = to_zs[shift_z] + to_ys[shift_y]
        send(outbox.at[chip], inbox.at[here], sems, {"region": chip * size_c + core})
    inbox[here] = outbox[here]

    others = pl.ds(0, chips - 1)
    whole = pltpu.make_async_remote_copy(
        src_ref=outbox.at[others],
        dst_ref=inbox.at[others],
        send_sem=sems[0],
        recv_sem=sems[1],
        device_id={"region": right},
        device_id_type=MESH,
    )
    whole.wait_recv()
    price_ref[...] = jnp.sum(inbox[...].astype(f32), axis=0)
    whole.wait_send()


def finish(angles, price, cleared, angles_hbm, payment_hbm, payment, sems):
    rows = angles.shape[0] // 8
    copies = [
        pltpu.make_async_copy(
            angles.at[pl.ds(i * rows, rows)], angles_hbm.at[pl.ds(i * rows, rows)], sems.at[i]
        )
        for i in range(8)
    ]
    for copy in copies:
        copy.start()
    payment[...] = cleared[...] * price[...]
    last = pltpu.make_async_copy(payment, payment_hbm, sems.at[8])
    last.start()
    for copy in copies:
        copy.wait()
    last.wait()


def settle(torus, *operands):
    (
        kkt_inverse,
        demand,
        cost_quad,
        cost_lin,
        capacity,
        ramp,
        gen_start,
        boundary_bus,
        tie_count,
        part_bus,
        part_share,
        cleared_mw,
    ) = operands
    hours, buses = demand.shape
    tie_slots = boundary_bus.shape[2]
    parts, taps = part_share.shape
    pieces = parts // LANES
    size_z, size_y, size_c = torus
    chunks = max(1, buses // 256)
    line = lambda value: value.reshape(1, -1)
    vmem = pl.BlockSpec(memory_space=pltpu.VMEM)
    hbm = pl.BlockSpec(memory_space=pltpu.HBM)
    bf16, f32, i32 = jnp.bfloat16, jnp.float32, jnp.int32
    dma = pltpu.SemaphoreType.DMA
    angles, price = pl.pallas_call(
        functools.partial(kernel, torus),
        out_shape=(
            jax.ShapeDtypeStruct((hours, buses), f32),
            jax.ShapeDtypeStruct((pieces, LANES), f32),
        ),
        in_specs=[hbm] * 11,
        out_specs=(vmem, vmem),
        scratch_shapes=[
            pltpu.VMEM((2, tie_slots), i32),
            pltpu.VMEM((1, tie_count.shape[0]), i32),
            pltpu.VMEM((hours, buses), f32),
            pltpu.VMEM((buses, buses), bf16),
            pltpu.VMEM((1, buses), f32),
            pltpu.VMEM((1, buses), f32),
            pltpu.VMEM((1, buses), f32),
            pltpu.VMEM((1, buses), f32),
            pltpu.VMEM((1, buses), f32),
            pltpu.VMEM((taps, parts), i32),
            pltpu.VMEM((taps, parts), f32),
            pltpu.VMEM((hours, buses), bf16),
            pltpu.VMEM((hours, buses), bf16),
            pltpu.VMEM((hours, buses), f32),
            pltpu.VMEM((hours, buses), f32),
            pltpu.VMEM((PAD + hours, buses), f32),
            pltpu.VMEM((hours, buses), f32),
            pltpu.VMEM((hours, buses), f32),
            pltpu.VMEM((1, buses), f32),
            pltpu.VMEM((buses, 2 * tie_slots), bf16),
            pltpu.VMEM((taps * (buses // LANES), 16, LANES), bf16),
            pltpu.VMEM((buses, parts), bf16),
            pltpu.VMEM((2, hours, tie_slots), bf16),
            pltpu.VMEM((2, hours, tie_slots), bf16),
            pltpu.VMEM((1, buses), f32),
            pltpu.VMEM((1, buses), f32),
            pltpu.VMEM((hours * pieces, LANES), f32),
            pltpu.VMEM((size_z * size_y, pieces, LANES), bf16),
            pltpu.VMEM((size_z * size_y, pieces, LANES), bf16),
            pltpu.VMEM((size_z * size_y, pieces, LANES), bf16),
            pltpu.VMEM((size_z * size_y, pieces, LANES), bf16),
            dma((10,)),
            dma((chunks,)),
            dma((2,)),
            dma((2,)),
            dma((2,)),
            pltpu.SemaphoreType.REGULAR,
            dma((2,)),
            dma((2,)),
        ],
        compiler_params=pltpu.CompilerParams(
            collective_id=0, has_side_effects=True, vmem_limit_bytes=16 * 1024 * 1024
        ),
    )(*[pltpu.with_memory_space_constraint(v, pltpu.HBM) for v in (
        boundary_bus[0],
        line(tie_count),
        demand,
        kkt_inverse,
        line(cost_quad),
        line(cost_lin),
        line(capacity),
        line(ramp),
        line(gen_start),
        part_bus.T,
        part_share.T,
    )])
    angles, payment = pl.pallas_call(
        finish,
        out_shape=(
            jax.ShapeDtypeStruct((hours, buses), f32),
            jax.ShapeDtypeStruct((pieces, LANES), f32),
        ),
        in_specs=[vmem] * 3,
        out_specs=(hbm, hbm),
        scratch_shapes=[pltpu.VMEM((pieces, LANES), f32), dma((9,))],
        compiler_params=pltpu.CompilerParams(vmem_limit_bytes=16 * 1024 * 1024),
    )(angles, price, cleared_mw.reshape(pieces, LANES))
    return angles, payment.reshape(cleared_mw.shape)


def solution(mesh, torus=(8, 8, 2)):
    return jax.shard_map(
        functools.partial(settle, torus),
        mesh=mesh,
        in_specs=(
            P("region", None, None),
            P("hour", "region"),
            P("region"),
            P("region"),
            P("region"),
            P("region"),
            P("region"),
            P("region", None, None),
            P(),
            P(),
            P(),
            P("hour", "region", None),
        ),
        out_specs=(P("hour", "region"), P("hour", "region", None)),
        check_vma=False,
    )
```

```python
import functools

import jax
import jax.numpy as jnp
from jax import lax
from jax.experimental import pallas as pl
from jax.experimental.pallas import tpu as pltpu
from jax.sharding import PartitionSpec as P

MESH = pl.DeviceIdType.MESH
NT = (((1,), (1,)), ((), ()))
LANES = 128
PAD = 8
GROUPS = 4


def far_first(size):
    return sorted(range(1, size), key=lambda shift: -min(shift, size - shift))


def far_first_all(torus):
    size_z, size_y, _ = torus
    shifts = [(a, b) for a in range(size_z) for b in range(size_y)]
    hops = lambda shift: min(shift[0], size_z - shift[0]) + min(shift[1], size_y - shift[1])
    return sorted(shifts[1:], key=lambda shift: -hops(shift))


def kernel(
    torus,
    boundary_hbm,
    tie_count_hbm,
    demand_hbm,
    kkt_hbm,
    cost_quad_hbm,
    cost_lin_hbm,
    capacity_hbm,
    ramp_hbm,
    gen_start_hbm,
    part_bus_hbm,
    part_share_hbm,
    angles_ref,
    price_ref,
    boundary,
    tie_count,
    demand,
    kkt,
    cost_quad,
    cost_lin,
    capacity,
    ramp,
    gen_start,
    part_bus,
    part_share,
    rhs,
    lmp,
    base,
    dual,
    gen,
    low_bound,
    high_bound,
    scale,
    slots,
    spread,
    shares,
    tie_out,
    tie_in,
    edge_out,
    edge_in,
    stage,
    pair_out,
    pair_in,
    outbox,
    inbox,
    load_sem,
    kkt_sem,
    tie_send,
    tie_recv,
    edge_sem,
    known,
    pair_sem,
    price_sem,
):
    size_z, size_y, size_c = torus
    regions = size_z * size_y * size_c
    region = lax.axis_index("region")
    block = lax.axis_index("hour")
    blocks = lax.axis_size("hour")
    z = region // (size_y * size_c)
    y = (region // size_c) % size_y
    core = region % size_c
    right = (region + 1) % regions
    left = (region + regions - 1) % regions
    later = (block + 1) % blocks
    earlier = (block + blocks - 1) % blocks
    hours, buses = demand.shape
    tie_slots = boundary.shape[1]
    chunk = min(256, buses)
    chunks = buses // chunk
    taps, parts = part_bus.shape
    pieces = parts // LANES
    f32, bf16 = jnp.float32, jnp.bfloat16

    def at(to_z, to_y, to_c):
        return {"region": (to_z * size_y + to_y) * size_c + to_c}

    def load(index, source, target):
        copy = pltpu.make_async_copy(source, target, load_sem.at[index])
        copy.start()
        return copy

    def send(source, target, sems, to):
        copy = pltpu.make_async_remote_copy(
            src_ref=source,
            dst_ref=target,
            send_sem=sems[0],
            recv_sem=sems[1],
            device_id=to,
            device_id_type=MESH,
        )
        copy.start()
        return copy

    slot_loads = [load(0, boundary_hbm, boundary), load(1, tie_count_hbm, tie_count)]
    demand_load = load(2, demand_hbm, demand)
    kkt_loads = []
    for c in range(chunks):
        copy = pltpu.make_async_copy(
            kkt_hbm.at[0, pl.ds(c * chunk, chunk)], kkt.at[pl.ds(c * chunk, chunk)], kkt_sem.at[c]
        )
        copy.start()
        kkt_loads.append(copy)
    pair_of = min(2, chunks)
    cost_loads = [
        load(3, cost_quad_hbm, cost_quad),
        load(4, cost_lin_hbm, cost_lin),
        load(5, capacity_hbm, capacity),
        load(6, ramp_hbm, ramp),
        load(7, gen_start_hbm, gen_start),
    ]
    part_loads = [load(8, part_bus_hbm, part_bus), load(9, part_share_hbm, part_share)]

    def along(step):
        ys = sorted({step % size_y, -step % size_y} - {0})
        zs = sorted({step % size_z, -step % size_z} - {0})
        return [at(z, (y + shift) % size_y, core) for shift in ys] + [
            at((z + shift) % size_z, y, core) for shift in zs
        ]

    def tell(sem, targets):
        for target in targets:
            pl.semaphore_signal(sem, inc=1, device_id=target, device_id_type=MESH)
        return len(targets)

    barrier = pltpu.get_barrier_semaphore()
    near = along(1) + [{"region": right}, {"region": left}]
    if blocks > 1:
        near = near + [{"hour": earlier}, {"hour": later}]
    greeted = tell(barrier, near)

    for copy in slot_loads:
        copy.wait()
    lane = lax.broadcasted_iota(jnp.int32, (1, tie_slots), 1)
    owner = lax.broadcasted_iota(jnp.int32, (1, regions), 1)
    row = lax.broadcasted_iota(jnp.int32, (chunk, tie_slots), 0)
    for side, edge_region in ((0, left), (1, region)):
        count = jnp.sum(
            jnp.where(owner == edge_region, tie_count[...], 0), axis=1, keepdims=True
        )
        bus = jnp.where(lane < count, boundary[pl.ds(side, 1), :], -1)
        for c in range(chunks):
            slots[pl.ds(c * chunk, chunk), pl.ds(side * tie_slots, tie_slots)] = jnp.where(
                row + c * chunk == bus, 1.0, 0.0
            ).astype(bf16)

    pl.semaphore_wait(barrier, greeted)
    told = tell(known.at[0], along(1))

    demand_load.wait()
    rhs[...] = demand[...].astype(bf16)
    for first in range(0, chunks, pair_of):
        for c in range(first, first + pair_of):
            kkt_loads[c].wait()
        both = [
            lax.dot_general(
                rhs[...], kkt[pl.ds(c * chunk, chunk), :], NT, preferred_element_type=f32
            )
            for c in range(first, first + pair_of)
        ]
        for c, angles in enumerate(both, first):
            angles_ref[:, pl.ds(c * chunk, chunk)] = angles
            part = jnp.dot(
                angles.astype(bf16),
                slots[pl.ds(c * chunk, chunk), :],
                preferred_element_type=f32,
            )
            ends = part if c == 0 else ends + part
    for side in range(2):
        tie_out[side] = ends[:, side * tie_slots : (side + 1) * tie_slots].astype(bf16)

    ties = [
        send(tie_out.at[1 - side], tie_in.at[side], (tie_send.at[side], tie_recv.at[side]), to)
        for side, to in ((0, {"region": right}), (1, {"region": left}))
    ]

    pl.semaphore_wait(known.at[0], told)
    told = tell(known.at[1], along(2))

    for copy in cost_loads:
        copy.wait()
    tall = min(32, hours)
    start_row = (lax.broadcasted_iota(jnp.int32, (tall, chunk), 0) == 0) & (block == 0)
    for c in range(chunks):
        cols = pl.ds(c * chunk, chunk)
        scale[:, cols] = 1.0 / (cost_quad[:, cols] + 1.0)
        for r in range(hours // tall):
            rows = pl.ds(r * tall, tall)
            angles = angles_ref[rows, cols]
            target = (angles - cost_lin[:, cols]) * scale[:, cols]
            if r == 0:
                prior = jnp.where(start_row, gen_start[:, cols], 0.0)
                limited = jnp.minimum(
                    jnp.maximum(target, prior - ramp[:, cols]), prior + ramp[:, cols]
                )
            else:
                limited = jnp.minimum(jnp.maximum(target, -ramp[:, cols]), ramp[:, cols])
            made = jnp.minimum(jnp.maximum(limited, 0.0), capacity[:, cols])
            owed = angles - made
            gen[pl.ds(PAD + r * tall, tall), cols] = made
            dual[rows, cols] = owed
            base[rows, cols] = demand[rows, cols] + (made - owed)
        edge_out[:, cols] = made[tall - 1 :, :]
        for r in range(hours // tall):
            rows = pl.ds(r * tall, tall)
            prior = gen[pl.ds(PAD - 1 + r * tall, tall), cols]
            top = capacity[:, cols]
            low_bound[rows, cols] = jnp.minimum(jnp.maximum(prior - ramp[:, cols], 0.0), top)
            high_bound[rows, cols] = jnp.minimum(jnp.maximum(prior + ramp[:, cols], 0.0), top)
    if blocks > 1:
        edge = send(edge_out, edge_in, (edge_sem.at[0], edge_sem.at[1]), {"hour": later})

    for copy in part_loads:
        copy.wait()
    high = buses // LANES
    tile = lax.broadcasted_iota(jnp.int32, (16, LANES), 0).astype(f32).astype(bf16)
    one, zero = jnp.ones((16, LANES), bf16), jnp.zeros((16, LANES), bf16)

    def fill(step, carry):
        cols = pl.ds(pl.multiple_of(step * LANES, LANES), LANES)
        low = []
        for k in range(taps):
            local = part_bus[pl.ds(k, 1), cols] - region * buses
            share = part_share[pl.ds(k, 1), cols]
            place = (local & (LANES - 1)).astype(f32)
            low.append(jnp.broadcast_to(place, (16, LANES)).astype(bf16))
            for i in range(high):
                held = jnp.where((local >> 7) == i, share, 0.0)
                spread[k * high + i] = jnp.broadcast_to(held, (16, LANES)).astype(bf16)
        for t in range(LANES // 16):
            place = tile + jnp.bfloat16(16 * t)
            ones = [jnp.where(place == low[k], one, zero) for k in range(taps)]
            for i in range(high):
                total = ones[0] * spread[i]
                for k in range(1, taps):
                    total = total + ones[k] * spread[k * high + i]
                shares[pl.ds(i * LANES + t * 16, 16), cols] = total
        return carry

    early = pieces * 8 // 8
    lax.fori_loop(0, early, fill, 0)
    if told:
        pl.semaphore_wait(known.at[1], told)
    row_peers = [at(z, (y + shift) % size_y, core) for shift in far_first(size_y)]
    told = tell(known.at[2], row_peers)
    lax.fori_loop(early, pieces, fill, 0)

    for copy in ties:
        copy.wait()
    for c in range(chunks):
        cols = pl.ds(c * chunk, chunk)
        tied = base[:, cols]
        for side in range(2):
            tied = tied + lax.dot_general(
                tie_in[side],
                slots[cols, pl.ds(side * tie_slots, tie_slots)],
                NT,
                preferred_element_type=f32,
            )
        rhs[:, cols] = tied.astype(bf16)

    prior = gen_start[...]
    if blocks > 1:
        edge.wait()
        prior = jnp.where(block == 0, prior, edge_in[...])
    low_bound[pl.ds(0, 1), :] = jnp.minimum(jnp.maximum(prior - ramp[...], 0.0), capacity[...])
    high_bound[pl.ds(0, 1), :] = jnp.minimum(jnp.maximum(prior + ramp[...], 0.0), capacity[...])
    for first in range(0, chunks, pair_of):
        for c in range(first, first + pair_of):
            cols = pl.ds(c * chunk, chunk)
            angles_ref[:, cols] = lax.dot_general(
                rhs[...], kkt[cols, :], NT, preferred_element_type=f32
            )
    for c in range(chunks):
        cols = pl.ds(c * chunk, chunk)
        for r in range(hours // tall):
            rows = pl.ds(r * tall, tall)
            owed = dual[rows, cols] + angles_ref[rows, cols]
            target = (owed - cost_lin[:, cols]) * scale[:, cols]
            made = jnp.minimum(jnp.maximum(target, low_bound[rows, cols]), high_bound[rows, cols])
            lmp[rows, cols] = (owed - made).astype(bf16)

    width = min(256, parts)
    for c in range(parts // width):
        part = jnp.dot(lmp[...], shares[:, pl.ds(c * width, width)], preferred_element_type=f32)
        for i in range(width // LANES):
            stage[pl.ds(c * (width // LANES) + i, hours, stride=pieces), :] = part[
                :, i * LANES : (i + 1) * LANES
            ]
    chips = size_z * size_y

    def priced(chip, owner):
        return stage[pl.ds(pl.multiple_of((chip * size_c + owner) * pieces, pieces), pieces), :]

    here = z * size_y + y
    to_zs = [(z + shift) % size_z * size_y for shift in range(size_z)]
    to_ys = [(y + shift) % size_y for shift in range(size_y)]
    targets = [to_zs[shift_z] + to_ys[shift_y] for shift_z, shift_y in far_first_all(torus)]
    farthest = targets[0]
    targets = [jnp.where(here == 0, farthest, 0)] + [
        jnp.where(chip == 0, farthest, chip) for chip in targets[1:]
    ]
    targets.append(here)
    group = max(1, chips // GROUPS)
    pairs = []
    for start in range(0, chips, group):
        for index in range(start, start + group):
            pair_out[index] = priced(targets[index], 1 - core).astype(bf16)
        some = pl.ds(start, group)
        pairs.append(
            send(
                pair_out.at[some],
                pair_in.at[some],
                (pair_sem.at[0, start // group], pair_sem.at[1, start // group]),
                at(z, y, 1 - core),
            )
        )
    pl.semaphore_wait(known.at[2], told)
    sems = (price_sem.at[0], price_sem.at[1])
    for start in range(0, chips, group):
        pairs[start // group].wait_recv()
        for index in range(start, start + group):
            mixed = priced(targets[index], core) + pair_in[index].astype(f32)
            outbox[index] = mixed.astype(bf16)
        for index in range(start, min(start + group, chips - 1)):
            to = {"region": targets[index] * size_c + core}
            send(outbox.at[index], inbox.at[here], sems, to)
    inbox[here] = outbox[chips - 1]
    for pair in pairs:
        pair.wait_send()

    others = pl.ds(0, chips - 1)
    whole = pltpu.make_async_remote_copy(
        src_ref=outbox.at[others],
        dst_ref=inbox.at[others],
        send_sem=sems[0],
        recv_sem=sems[1],
        device_id={"region": right},
        device_id_type=MESH,
    )
    whole.wait_recv()
    price_ref[...] = jnp.sum(inbox[...].astype(f32), axis=0)
    whole.wait_send()


def finish(angles, price, cleared, angles_hbm, payment_hbm, payment, sems):
    rows = angles.shape[0] // 8
    copies = [
        pltpu.make_async_copy(
            angles.at[pl.ds(i * rows, rows)], angles_hbm.at[pl.ds(i * rows, rows)], sems.at[i]
        )
        for i in range(8)
    ]
    for copy in copies:
        copy.start()
    payment[...] = cleared[...] * price[...]
    last = pltpu.make_async_copy(payment, payment_hbm, sems.at[8])
    last.start()
    for copy in copies:
        copy.wait()
    last.wait()


def settle(torus, *operands):
    (
        kkt_inverse,
        demand,
        cost_quad,
        cost_lin,
        capacity,
        ramp,
        gen_start,
        boundary_bus,
        tie_count,
        part_bus,
        part_share,
        cleared_mw,
    ) = operands
    hours, buses = demand.shape
    tie_slots = boundary_bus.shape[2]
    parts, taps = part_share.shape
    pieces = parts // LANES
    size_z, size_y, size_c = torus
    chunks = max(1, buses // 256)
    line = lambda value: value.reshape(1, -1)
    vmem = pl.BlockSpec(memory_space=pltpu.VMEM)
    hbm = pl.BlockSpec(memory_space=pltpu.HBM)
    bf16, f32, i32 = jnp.bfloat16, jnp.float32, jnp.int32
    dma = pltpu.SemaphoreType.DMA
    angles, price = pl.pallas_call(
        functools.partial(kernel, torus),
        out_shape=(
            jax.ShapeDtypeStruct((hours, buses), f32),
            jax.ShapeDtypeStruct((pieces, LANES), f32),
        ),
        in_specs=[hbm] * 11,
        out_specs=(vmem, vmem),
        scratch_shapes=[
            pltpu.VMEM((2, tie_slots), i32),
            pltpu.VMEM((1, tie_count.shape[0]), i32),
            pltpu.VMEM((hours, buses), f32),
            pltpu.VMEM((buses, buses), bf16),
            pltpu.VMEM((1, buses), f32),
            pltpu.VMEM((1, buses), f32),
            pltpu.VMEM((1, buses), f32),
            pltpu.VMEM((1, buses), f32),
            pltpu.VMEM((1, buses), f32),
            pltpu.VMEM((taps, parts), i32),
            pltpu.VMEM((taps, parts), f32),
            pltpu.VMEM((hours, buses), bf16),
            pltpu.VMEM((hours, buses), bf16),
            pltpu.VMEM((hours, buses), f32),
            pltpu.VMEM((hours, buses), f32),
            pltpu.VMEM((PAD + hours, buses), f32),
            pltpu.VMEM((hours, buses), f32),
            pltpu.VMEM((hours, buses), f32),
            pltpu.VMEM((1, buses), f32),
            pltpu.VMEM((buses, 2 * tie_slots), bf16),
            pltpu.VMEM((taps * (buses // LANES), 16, LANES), bf16),
            pltpu.VMEM((buses, parts), bf16),
            pltpu.VMEM((2, hours, tie_slots), bf16),
            pltpu.VMEM((2, hours, tie_slots), bf16),
            pltpu.VMEM((1, buses), f32),
            pltpu.VMEM((1, buses), f32),
            pltpu.VMEM((hours * pieces, LANES), f32),
            pltpu.VMEM((size_z * size_y, pieces, LANES), bf16),
            pltpu.VMEM((size_z * size_y, pieces, LANES), bf16),
            pltpu.VMEM((size_z * size_y, pieces, LANES), bf16),
            pltpu.VMEM((size_z * size_y, pieces, LANES), bf16),
            dma((10,)),
            dma((chunks,)),
            dma((2,)),
            dma((2,)),
            dma((2,)),
            pltpu.SemaphoreType.REGULAR((3,)),
            dma((2, GROUPS)),
            dma((2,)),
        ],
        compiler_params=pltpu.CompilerParams(
            collective_id=0, has_side_effects=True, vmem_limit_bytes=16 * 1024 * 1024
        ),
    )(*[pltpu.with_memory_space_constraint(v, pltpu.HBM) for v in (
        boundary_bus[0],
        line(tie_count),
        demand,
        kkt_inverse,
        line(cost_quad),
        line(cost_lin),
        line(capacity),
        line(ramp),
        line(gen_start),
        part_bus.T,
        part_share.T,
    )])
    angles, payment = pl.pallas_call(
        finish,
        out_shape=(
            jax.ShapeDtypeStruct((hours, buses), f32),
            jax.ShapeDtypeStruct((pieces, LANES), f32),
        ),
        in_specs=[vmem] * 3,
        out_specs=(hbm, hbm),
        scratch_shapes=[pltpu.VMEM((pieces, LANES), f32), dma((9,))],
        compiler_params=pltpu.CompilerParams(vmem_limit_bytes=16 * 1024 * 1024),
    )(angles, price, cleared_mw.reshape(pieces, LANES))
    return angles, payment.reshape(cleared_mw.shape)


def solution(mesh, torus=(8, 8, 2)):
    return jax.shard_map(
        functools.partial(settle, torus),
        mesh=mesh,
        in_specs=(
            P("region", None, None),
            P("hour", "region"),
            P("region"),
            P("region"),
            P("region"),
            P("region"),
            P("region"),
            P("region", None, None),
            P(),
            P(),
            P(),
            P("hour", "region", None),
        ),
        out_specs=(P("hour", "region"), P("hour", "region", None)),
        check_vma=False,
    )
```

```python
import functools

import jax
import jax.numpy as jnp
from jax import lax
from jax.experimental import pallas as pl
from jax.experimental.pallas import tpu as pltpu
from jax.sharding import PartitionSpec as P

MESH = pl.DeviceIdType.MESH
NT = (((1,), (1,)), ((), ()))
LANES = 128
PAD = 8
GROUPS = 4


def far_first(size):
    return sorted(range(1, size), key=lambda shift: -min(shift, size - shift))


def far_first_all(torus):
    size_z, size_y, _ = torus
    shifts = [(a, b) for a in range(size_z) for b in range(size_y)]
    hops = lambda shift: min(shift[0], size_z - shift[0]) + min(shift[1], size_y - shift[1])
    return sorted(shifts[1:], key=lambda shift: -hops(shift))


def kernel(
    torus,
    boundary_hbm,
    tie_count_hbm,
    demand_hbm,
    kkt_hbm,
    cost_quad_hbm,
    cost_lin_hbm,
    capacity_hbm,
    ramp_hbm,
    gen_start_hbm,
    part_bus_hbm,
    part_share_hbm,
    angles_ref,
    price_ref,
    boundary,
    tie_count,
    demand,
    kkt,
    cost_quad,
    cost_lin,
    capacity,
    ramp,
    gen_start,
    part_bus,
    part_share,
    rhs,
    lmp,
    base,
    dual,
    gen,
    low_bound,
    high_bound,
    scale,
    slots,
    spread,
    shares,
    tie_out,
    tie_in,
    edge_out,
    edge_in,
    stage,
    pair_out,
    pair_in,
    outbox,
    inbox,
    load_sem,
    kkt_sem,
    tie_send,
    tie_recv,
    edge_sem,
    known,
    pair_sem,
    price_sem,
):
    size_z, size_y, size_c = torus
    regions = size_z * size_y * size_c
    region = lax.axis_index("region")
    block = lax.axis_index("hour")
    blocks = lax.axis_size("hour")
    z = region // (size_y * size_c)
    y = (region // size_c) % size_y
    core = region % size_c
    right = (region + 1) % regions
    left = (region + regions - 1) % regions
    later = (block + 1) % blocks
    earlier = (block + blocks - 1) % blocks
    hours, buses = demand.shape
    tie_slots = boundary.shape[1]
    chunk = min(256, buses)
    chunks = buses // chunk
    taps, parts = part_bus.shape
    pieces = parts // LANES
    f32, bf16 = jnp.float32, jnp.bfloat16

    def at(to_z, to_y, to_c):
        return {"region": (to_z * size_y + to_y) * size_c + to_c}

    def load(index, source, target):
        copy = pltpu.make_async_copy(source, target, load_sem.at[index])
        copy.start()
        return copy

    def send(source, target, sems, to):
        copy = pltpu.make_async_remote_copy(
            src_ref=source,
            dst_ref=target,
            send_sem=sems[0],
            recv_sem=sems[1],
            device_id=to,
            device_id_type=MESH,
        )
        copy.start()
        return copy

    slot_loads = [load(0, boundary_hbm, boundary), load(1, tie_count_hbm, tie_count)]
    demand_load = load(2, demand_hbm, demand)
    kkt_loads = []
    for c in range(chunks):
        copy = pltpu.make_async_copy(
            kkt_hbm.at[0, pl.ds(c * chunk, chunk)], kkt.at[pl.ds(c * chunk, chunk)], kkt_sem.at[c]
        )
        copy.start()
        kkt_loads.append(copy)
    pair_of = min(2, chunks)
    cost_loads = [
        load(3, cost_quad_hbm, cost_quad),
        load(4, cost_lin_hbm, cost_lin),
        load(5, capacity_hbm, capacity),
        load(6, ramp_hbm, ramp),
        load(7, gen_start_hbm, gen_start),
    ]
    part_loads = [load(8, part_bus_hbm, part_bus), load(9, part_share_hbm, part_share)]

    def along(step):
        ys = sorted({step % size_y, -step % size_y} - {0})
        zs = sorted({step % size_z, -step % size_z} - {0})
        return [at(z, (y + shift) % size_y, core) for shift in ys] + [
            at((z + shift) % size_z, y, core) for shift in zs
        ]

    def tell(sem, targets):
        for target in targets:
            pl.semaphore_signal(sem, inc=1, device_id=target, device_id_type=MESH)
        return len(targets)

    barrier = pltpu.get_barrier_semaphore()
    near = along(1) + [{"region": right}, {"region": left}]
    if blocks > 1:
        near = near + [{"hour": earlier}, {"hour": later}]
    greeted = tell(barrier, near)

    for copy in slot_loads:
        copy.wait()
    lane = lax.broadcasted_iota(jnp.int32, (1, tie_slots), 1)
    owner = lax.broadcasted_iota(jnp.int32, (1, regions), 1)
    row = lax.broadcasted_iota(jnp.int32, (chunk, tie_slots), 0)
    for side, edge_region in ((0, left), (1, region)):
        count = jnp.sum(
            jnp.where(owner == edge_region, tie_count[...], 0), axis=1, keepdims=True
        )
        bus = jnp.where(lane < count, boundary[pl.ds(side, 1), :], -1)
        for c in range(chunks):
            slots[pl.ds(c * chunk, chunk), pl.ds(side * tie_slots, tie_slots)] = jnp.where(
                row + c * chunk == bus, 1.0, 0.0
            ).astype(bf16)

    pl.semaphore_wait(barrier, greeted)
    told = tell(known.at[0], along(1))

    demand_load.wait()
    rhs[...] = demand[...].astype(bf16)
    for first in range(0, chunks, pair_of):
        for c in range(first, first + pair_of):
            kkt_loads[c].wait()
        both = [
            lax.dot_general(
                rhs[...], kkt[pl.ds(c * chunk, chunk), :], NT, preferred_element_type=f32
            )
            for c in range(first, first + pair_of)
        ]
        for c, angles in enumerate(both, first):
            angles_ref[:, pl.ds(c * chunk, chunk)] = angles
            part = jnp.dot(
                angles.astype(bf16),
                slots[pl.ds(c * chunk, chunk), :],
                preferred_element_type=f32,
            )
            ends = part if c == 0 else ends + part
    for side in range(2):
        tie_out[side] = ends[:, side * tie_slots : (side + 1) * tie_slots].astype(bf16)

    ties = [
        send(tie_out.at[1 - side], tie_in.at[side], (tie_send.at[side], tie_recv.at[side]), to)
        for side, to in ((0, {"region": right}), (1, {"region": left}))
    ]

    for copy in cost_loads:
        copy.wait()
    tall = min(32, hours)
    start_row = (lax.broadcasted_iota(jnp.int32, (tall, chunk), 0) == 0) & (block == 0)
    for c in range(chunks):
        cols = pl.ds(c * chunk, chunk)
        scale[:, cols] = 1.0 / (cost_quad[:, cols] + 1.0)
        for r in range(hours // tall):
            rows = pl.ds(r * tall, tall)
            angles = angles_ref[rows, cols]
            target = (angles - cost_lin[:, cols]) * scale[:, cols]
            if r == 0:
                prior = jnp.where(start_row, gen_start[:, cols], 0.0)
                limited = jnp.minimum(
                    jnp.maximum(target, prior - ramp[:, cols]), prior + ramp[:, cols]
                )
            else:
                limited = jnp.minimum(jnp.maximum(target, -ramp[:, cols]), ramp[:, cols])
            made = jnp.minimum(jnp.maximum(limited, 0.0), capacity[:, cols])
            owed = angles - made
            gen[pl.ds(PAD + r * tall, tall), cols] = made
            dual[rows, cols] = owed
            base[rows, cols] = demand[rows, cols] + (made - owed)
        edge_out[:, cols] = made[tall - 1 :, :]
        for r in range(hours // tall):
            rows = pl.ds(r * tall, tall)
            prior = gen[pl.ds(PAD - 1 + r * tall, tall), cols]
            top = capacity[:, cols]
            low_bound[rows, cols] = jnp.minimum(jnp.maximum(prior - ramp[:, cols], 0.0), top)
            high_bound[rows, cols] = jnp.minimum(jnp.maximum(prior + ramp[:, cols], 0.0), top)
    if blocks > 1:
        edge = send(edge_out, edge_in, (edge_sem.at[0], edge_sem.at[1]), {"hour": later})

    pl.semaphore_wait(known.at[0], told)
    told = tell(known.at[1], along(2))

    for copy in part_loads:
        copy.wait()
    high = buses // LANES
    tile = lax.broadcasted_iota(jnp.int32, (16, LANES), 0).astype(f32).astype(bf16)
    one, zero = jnp.ones((16, LANES), bf16), jnp.zeros((16, LANES), bf16)

    def fill(step, carry):
        cols = pl.ds(pl.multiple_of(step * LANES, LANES), LANES)
        low = []
        for k in range(taps):
            local = part_bus[pl.ds(k, 1), cols] - region * buses
            share = part_share[pl.ds(k, 1), cols]
            place = (local & (LANES - 1)).astype(f32)
            low.append(jnp.broadcast_to(place, (16, LANES)).astype(bf16))
            for i in range(high):
                held = jnp.where((local >> 7) == i, share, 0.0)
                spread[k * high + i] = jnp.broadcast_to(held, (16, LANES)).astype(bf16)
        for t in range(LANES // 16):
            place = tile + jnp.bfloat16(16 * t)
            ones = [jnp.where(place == low[k], one, zero) for k in range(taps)]
            for i in range(high):
                total = ones[0] * spread[i]
                for k in range(1, taps):
                    total = total + ones[k] * spread[k * high + i]
                shares[pl.ds(i * LANES + t * 16, 16), cols] = total
        return carry

    early = pieces * 8 // 8
    lax.fori_loop(0, early, fill, 0)
    if told:
        pl.semaphore_wait(known.at[1], told)
    row_peers = [at(z, (y + shift) % size_y, core) for shift in far_first(size_y)]
    told = tell(known.at[2], row_peers)
    lax.fori_loop(early, pieces, fill, 0)

    for copy in ties:
        copy.wait()
    for c in range(chunks):
        cols = pl.ds(c * chunk, chunk)
        tied = base[:, cols]
        for side in range(2):
            tied = tied + lax.dot_general(
                tie_in[side],
                slots[cols, pl.ds(side * tie_slots, tie_slots)],
                NT,
                preferred_element_type=f32,
            )
        rhs[:, cols] = tied.astype(bf16)

    prior = gen_start[...]
    if blocks > 1:
        edge.wait()
        prior = jnp.where(block == 0, prior, edge_in[...])
    low_bound[pl.ds(0, 1), :] = jnp.minimum(jnp.maximum(prior - ramp[...], 0.0), capacity[...])
    high_bound[pl.ds(0, 1), :] = jnp.minimum(jnp.maximum(prior + ramp[...], 0.0), capacity[...])
    for first in range(0, chunks, pair_of):
        for c in range(first, first + pair_of):
            cols = pl.ds(c * chunk, chunk)
            angles_ref[:, cols] = lax.dot_general(
                rhs[...], kkt[cols, :], NT, preferred_element_type=f32
            )
    for c in range(chunks):
        cols = pl.ds(c * chunk, chunk)
        for r in range(hours // tall):
            rows = pl.ds(r * tall, tall)
            owed = dual[rows, cols] + angles_ref[rows, cols]
            target = (owed - cost_lin[:, cols]) * scale[:, cols]
            made = jnp.minimum(jnp.maximum(target, low_bound[rows, cols]), high_bound[rows, cols])
            lmp[rows, cols] = (owed - made).astype(bf16)

    width = min(256, parts)
    for c in range(parts // width):
        part = jnp.dot(lmp[...], shares[:, pl.ds(c * width, width)], preferred_element_type=f32)
        for i in range(width // LANES):
            stage[pl.ds(c * (width // LANES) + i, hours, stride=pieces), :] = part[
                :, i * LANES : (i + 1) * LANES
            ]
    chips = size_z * size_y

    def priced(chip, owner):
        return stage[pl.ds(pl.multiple_of((chip * size_c + owner) * pieces, pieces), pieces), :]

    here = z * size_y + y
    to_zs = [(z + shift) % size_z * size_y for shift in range(size_z)]
    to_ys = [(y + shift) % size_y for shift in range(size_y)]
    targets = [to_zs[shift_z] + to_ys[shift_y] for shift_z, shift_y in far_first_all(torus)]
    farthest = targets[0]
    targets = [jnp.where(here == 0, farthest, 0)] + [
        jnp.where(chip == 0, farthest, chip) for chip in targets[1:]
    ]
    targets.append(here)
    group = max(1, chips // GROUPS)
    pairs = []
    for start in range(0, chips, group):
        for index in range(start, start + group):
            pair_out[index] = priced(targets[index], 1 - core).astype(bf16)
        some = pl.ds(start, group)
        pairs.append(
            send(
                pair_out.at[some],
                pair_in.at[some],
                (pair_sem.at[0, start // group], pair_sem.at[1, start // group]),
                at(z, y, 1 - core),
            )
        )
    pl.semaphore_wait(known.at[2], told)
    sems = (price_sem.at[0], price_sem.at[1])
    for start in range(0, chips, group):
        pairs[start // group].wait_recv()
        for index in range(start, start + group):
            mixed = priced(targets[index], core) + pair_in[index].astype(f32)
            outbox[index] = mixed.astype(bf16)
        for index in range(start, min(start + group, chips - 1)):
            to = {"region": targets[index] * size_c + core}
            send(outbox.at[index], inbox.at[here], sems, to)
    inbox[here] = outbox[chips - 1]
    for pair in pairs:
        pair.wait_send()

    others = pl.ds(0, chips - 1)
    whole = pltpu.make_async_remote_copy(
        src_ref=outbox.at[others],
        dst_ref=inbox.at[others],
        send_sem=sems[0],
        recv_sem=sems[1],
        device_id={"region": right},
        device_id_type=MESH,
    )
    whole.wait_recv()
    price_ref[...] = jnp.sum(inbox[...].astype(f32), axis=0)
    whole.wait_send()


def finish(angles, price, cleared, angles_hbm, payment_hbm, payment, sems):
    rows = angles.shape[0] // 8
    copies = [
        pltpu.make_async_copy(
            angles.at[pl.ds(i * rows, rows)], angles_hbm.at[pl.ds(i * rows, rows)], sems.at[i]
        )
        for i in range(8)
    ]
    for copy in copies:
        copy.start()
    payment[...] = cleared[...] * price[...]
    last = pltpu.make_async_copy(payment, payment_hbm, sems.at[8])
    last.start()
    for copy in copies:
        copy.wait()
    last.wait()


def settle(torus, *operands):
    (
        kkt_inverse,
        demand,
        cost_quad,
        cost_lin,
        capacity,
        ramp,
        gen_start,
        boundary_bus,
        tie_count,
        part_bus,
        part_share,
        cleared_mw,
    ) = operands
    hours, buses = demand.shape
    tie_slots = boundary_bus.shape[2]
    parts, taps = part_share.shape
    pieces = parts // LANES
    size_z, size_y, size_c = torus
    chunks = max(1, buses // 256)
    line = lambda value: value.reshape(1, -1)
    vmem = pl.BlockSpec(memory_space=pltpu.VMEM)
    hbm = pl.BlockSpec(memory_space=pltpu.HBM)
    bf16, f32, i32 = jnp.bfloat16, jnp.float32, jnp.int32
    dma = pltpu.SemaphoreType.DMA
    angles, price = pl.pallas_call(
        functools.partial(kernel, torus),
        out_shape=(
            jax.ShapeDtypeStruct((hours, buses), f32),
            jax.ShapeDtypeStruct((pieces, LANES), f32),
        ),
        in_specs=[hbm] * 11,
        out_specs=(vmem, vmem),
        scratch_shapes=[
            pltpu.VMEM((2, tie_slots), i32),
            pltpu.VMEM((1, tie_count.shape[0]), i32),
            pltpu.VMEM((hours, buses), f32),
            pltpu.VMEM((buses, buses), bf16),
            pltpu.VMEM((1, buses), f32),
            pltpu.VMEM((1, buses), f32),
            pltpu.VMEM((1, buses), f32),
            pltpu.VMEM((1, buses), f32),
            pltpu.VMEM((1, buses), f32),
            pltpu.VMEM((taps, parts), i32),
            pltpu.VMEM((taps, parts), f32),
            pltpu.VMEM((hours, buses), bf16),
            pltpu.VMEM((hours, buses), bf16),
            pltpu.VMEM((hours, buses), f32),
            pltpu.VMEM((hours, buses), f32),
            pltpu.VMEM((PAD + hours, buses), f32),
            pltpu.VMEM((hours, buses), f32),
            pltpu.VMEM((hours, buses), f32),
            pltpu.VMEM((1, buses), f32),
            pltpu.VMEM((buses, 2 * tie_slots), bf16),
            pltpu.VMEM((taps * (buses // LANES), 16, LANES), bf16),
            pltpu.VMEM((buses, parts), bf16),
            pltpu.VMEM((2, hours, tie_slots), bf16),
            pltpu.VMEM((2, hours, tie_slots), bf16),
            pltpu.VMEM((1, buses), f32),
            pltpu.VMEM((1, buses), f32),
            pltpu.VMEM((hours * pieces, LANES), f32),
            pltpu.VMEM((size_z * size_y, pieces, LANES), bf16),
            pltpu.VMEM((size_z * size_y, pieces, LANES), bf16),
            pltpu.VMEM((size_z * size_y, pieces, LANES), bf16),
            pltpu.VMEM((size_z * size_y, pieces, LANES), bf16),
            dma((10,)),
            dma((chunks,)),
            dma((2,)),
            dma((2,)),
            dma((2,)),
            pltpu.SemaphoreType.REGULAR((3,)),
            dma((2, GROUPS)),
            dma((2,)),
        ],
        compiler_params=pltpu.CompilerParams(
            collective_id=0, has_side_effects=True, vmem_limit_bytes=16 * 1024 * 1024
        ),
    )(*[pltpu.with_memory_space_constraint(v, pltpu.HBM) for v in (
        boundary_bus[0],
        line(tie_count),
        demand,
        kkt_inverse,
        line(cost_quad),
        line(cost_lin),
        line(capacity),
        line(ramp),
        line(gen_start),
        part_bus.T,
        part_share.T,
    )])
    angles, payment = pl.pallas_call(
        finish,
        out_shape=(
            jax.ShapeDtypeStruct((hours, buses), f32),
            jax.ShapeDtypeStruct((pieces, LANES), f32),
        ),
        in_specs=[vmem] * 3,
        out_specs=(hbm, hbm),
        scratch_shapes=[pltpu.VMEM((pieces, LANES), f32), dma((9,))],
        compiler_params=pltpu.CompilerParams(vmem_limit_bytes=16 * 1024 * 1024),
    )(angles, price, cleared_mw.reshape(pieces, LANES))
    return angles, payment.reshape(cleared_mw.shape)


def solution(mesh, torus=(8, 8, 2)):
    return jax.shard_map(
        functools.partial(settle, torus),
        mesh=mesh,
        in_specs=(
            P("region", None, None),
            P("hour", "region"),
            P("region"),
            P("region"),
            P("region"),
            P("region"),
            P("region"),
            P("region", None, None),
            P(),
            P(),
            P(),
            P("hour", "region", None),
        ),
        out_specs=(P("hour", "region"), P("hour", "region", None)),
        check_vma=False,
    )
```
